32 devices in a mesh: py: 8 (over y, x, core), pz: 4 (over z).
Axes of the slice: x: 2, y: 2, z: 4, core: 2. Of those that a mesh axis runs over, the one named last changes fastest.
Arguments:
- velocity: float32 [3, 32, 128, 2048], P(None, ('py', 'pz')), may hold values from -6 to 6
- fluid: float32 [32, 128, 2048], P(('py', 'pz')), may hold values from 0.1 to 1
- pressure: float32 [32, 128, 2048], P(None, 'pz', 'py'), may hold values from -4 to 4
Outputs:
- projected: float32 [3, 32, 128, 2048], P(None, ('py', 'pz'))
- divergence: float32 [32, 128, 2048], P(None, 'pz', 'py')
The draws below stay inside these ranges and needn't reach their ends.
All inputs are finite; a program needn't handle non-finite values.
Results may differ from the reference program's by a relative error of at most 0.00002.
Values sent between devices are 32-bit elements; how exact they have to be, the bound alone decides.
A program may use at most 64 MiB of HBM per device.

```python
import jax
import jax.numpy as jnp
from jax import lax

NY = 2048
NZ = 128
NX = 32


def shard_levels(rng, shape, shards, low, high):
    loudness, own = 1.0, jax.random.fold_in(rng, 6)
    for dim, shards_of in shards:
        draws = jnp.exp(jax.random.uniform(jax.random.fold_in(own, dim), (shards_of,), jnp.float32, low / len(shards), high / len(shards)))
        loudness = loudness * jnp.repeat(draws, shape[dim] // shards_of).reshape([-1 if axis == dim else 1 for axis in range(len(shape))])
    return loudness


def bell_draw(key, shape, deviation, limit, cuts=(), held_as=jnp.bfloat16):
    array = jax.random.normal(key, shape, jnp.float32) * deviation
    if len(cuts) > 0:
        array = shard_levels(key, shape, cuts, -0.22, 0.18) * array
    return jnp.clip(array, min=-limit, max=limit).astype(held_as)


def setup_inputs(seed: int = 0) -> dict:
    splits = jax.random.split(jax.random.key(seed), 4)
    velocity = bell_draw(splits[0], (3, NX, NZ, NY), 1.0, 6.0, ((1, 32),), jnp.float32)
    fluid = jnp.clip(0.1 + 0.9 * jax.random.uniform(splits[1], (NX, NZ, NY), jnp.float32) ** shard_levels(splits[1], (NX, NZ, NY), ((0, 32),), -0.2, 0.2), 0.1, 1.0)
    pressure = bell_draw(splits[2], (NX, NZ, NY), 0.5, 4.0, ((1, 4), (2, 8)), jnp.float32)
    return {"velocity": velocity, "fluid": fluid, "pressure": pressure}


def face_update(component, fluid, pressure, axis):
    index = lax.broadcasted_iota(jnp.int32, fluid.shape, axis)
    fluid_prev = jnp.roll(fluid, 1, axis)
    pressure_prev = jnp.roll(pressure, 1, axis)
    weight = jnp.where(index == 0, jnp.float32(0.0), 0.5 * (fluid + fluid_prev))
    return weight * (component - (pressure - pressure_prev))


def forward_difference(updated, axis):
    index = lax.broadcasted_iota(jnp.int32, updated.shape, axis)
    following = jnp.where(index == updated.shape[axis] - 1, jnp.float32(0.0), jnp.roll(updated, -1, axis))
    return following - updated


def reference(velocity, fluid, pressure):
    parts = []
    divergence = jnp.zeros(fluid.shape, jnp.float32)
    for axis in range(3):
        updated = face_update(velocity[axis], fluid, pressure, axis)
        divergence = divergence + forward_difference(updated, axis)
        parts.append(updated)
    return jnp.stack(parts, 0), divergence
```

```python
import functools

import jax
import jax.numpy as jnp
from jax import lax
from jax.experimental import pallas as pl
from jax.experimental.pallas import tpu as pltpu
from jax.sharding import PartitionSpec as P

AHEAD = 2
AHEAD_F = 1
LANES = 128


def kernel(
    count_y, count_z, v_hbm, f_hbm, p_hbm, out_ref, div,
    v, f, f_low, main, halo, left, part, next_x, got, got_x,
    in_sem,
    main_s, main_r, halo_s, halo_r, edge_s, edge_r, f_s, f_r, fwd_s, fwd_r, nx_s, nx_r,
    a_s, a_r, x_s, x_r,
):
    out = out_ref.at[:, 0]
    py = lax.axis_index("py")
    pz = lax.axis_index("pz")
    me = py * count_z + pz
    planes = count_y * count_z
    rows, across = f.shape
    width = across // count_y
    part_rows = rows // count_z
    half = count_z // 2 if count_z % 2 == 0 else 1

    def side(z):
        return z // half if isinstance(z, int) else lax.div(z, half)

    def joined(z):
        return min((z + 1) % half, 1) if isinstance(z, int) else jnp.minimum(lax.rem(z + 1, half), 1)

    def cols(c):
        return pl.ds(pl.multiple_of(c * width, width), width)

    def band(g):
        return pl.ds(g * part_rows, part_rows)

    def wrap(c):
        return lax.rem(c + 2 * count_y, count_y)

    def remote(src, dst, send, recv, y, z):
        return pltpu.make_async_remote_copy(
            src_ref=src, dst_ref=dst, send_sem=send, recv_sem=recv,
            device_id=(y, z), device_id_type=pl.DeviceIdType.MESH,
        )

    def begin(src, dst, send, recv, y, z, gate=1, away=False):
        apart = 1 if away else jnp.abs(y * count_z + z - me)

        @pl.when(jnp.minimum(gate, apart) > 0)
        def _():
            remote(src, dst, send, recv, y, z).start()

        if not away:
            @pl.when(gate - jnp.minimum(apart, 1) > 0)
            def _():
                pltpu.make_async_copy(src, dst, recv).start()

    def sent(src, dst, send, recv, y, z, gate=1, away=False):
        apart = 1 if away else jnp.abs(y * count_z + z - me)

        @pl.when(jnp.minimum(gate, apart) > 0)
        def _():
            remote(src, dst, send, recv, y, z).wait_send()

    def landed(dst, recv):
        pltpu.make_async_copy(dst, dst, recv).wait()

    def passed(z, g):
        low, high = (min, max) if isinstance(z, int) and isinstance(g, int) else (jnp.minimum, jnp.maximum)
        apart = low(high(abs(g - z) - 1, 0), 1)
        across_middle = joined(z - 1) * low(abs(side(g) - side(z)), 1)
        return low(high(apart, across_middle), low(z, 1))

    def passed_up(z, g):
        return passed(z + 1, g) if isinstance(z, int) and z < count_z - 1 else (
            0 if isinstance(z, int) else jnp.minimum(passed(z + 1, g), count_z - 1 - z))

    loads = [
        pltpu.make_async_copy(v_hbm.at[:, 0], v, in_sem.at[0]),
        pltpu.make_async_copy(f_hbm.at[0], f, in_sem.at[1]),
    ]
    for load in loads:
        load.start()

    barrier = pltpu.get_barrier_semaphore()

    def greet(i, carry):
        @pl.when(i != me)
        def _():
            pl.semaphore_signal(
                barrier, inc=1, device_id=(lax.div(i, count_z), lax.rem(i, count_z)),
                device_id_type=pl.DeviceIdType.MESH,
            )
        return carry

    lax.fori_loop(0, planes, greet, 0)
    pl.semaphore_wait(barrier, planes - 1)

    mine = pl.ds(pl.multiple_of(pz * part_rows, part_rows), part_rows)
    ahead_y = lax.div(me + 1, count_z)
    ahead_z = lax.rem(me + 1, count_z)

    def pressure_sends(k, do):
        y = wrap(py - k)
        for z in range(count_z):
            target = y * count_z + z
            slot = k * count_z + z
            do(p_hbm.at[target], main.at[mine, cols(py)], main_s.at[slot], main_r.at[k * count_z + pz], y, z)

            do(p_hbm.at[jnp.maximum(target - 1, 0)], halo.at[mine, cols(py)],
               halo_s.at[slot], halo_r.at[k * count_z + pz], y, z, gate=1 - passed(z, pz))

    def fluid_sends(k, do):
        c = cols(wrap(ahead_y + k))
        do(f_hbm.at[0, :, c], f_low.at[:, c], f_s.at[k], f_r.at[k], ahead_y, ahead_z,
           gate=planes - 1 - me, away=True)

    def edge_sends(do):
        for z in range(count_z):
            y = wrap(py + 1)
            do(p_hbm.at[y * count_z + z, :, width - LANES:], left.at[mine],
               edge_s.at[z], edge_r.at[pz], y, z, away=True)

    def forward(k, do):
        c = cols(wrap(py + k))
        for g in range(count_z):
            slot = k * count_z + g
            do(main.at[band(g), c], halo.at[band(g), c], fwd_s.at[slot], fwd_r.at[slot], py, pz + 1,
               gate=passed_up(pz, g), away=True)

    def lend(k, do):
        c = cols(wrap(py + k))
        for g in range(count_z):
            slot = k * count_z + g
            do(out.at[0, band(g), c], next_x.at[band(g), c], nx_s.at[slot], nx_r.at[slot], py, pz - 1,
               gate=passed(pz, g), away=True)

    def result_sends(k, do):
        y = wrap(py + k)
        for z in range(count_z):
            slot = k * count_z + z
            do(part.at[band(z), cols(y)], got.at[me], a_s.at[slot], a_r.at[me], y, z)
            below = jnp.maximum(me - 1, 0)
            do(out.at[0, band(z), cols(y)], got_x.at[below], x_s.at[slot], x_r.at[below], y, z,
               gate=jnp.minimum(me, 1 - passed(pz, z)))

    edge_sends(begin)
    for k in range(min(AHEAD, count_y)):
        pressure_sends(k, begin)
    for k in range(min(AHEAD_F, count_y)):
        fluid_sends(k, begin)
    for load in loads:
        load.wait()
    for z in range(count_z):
        landed(left.at[band(z)], edge_r.at[z])

    def before(tile, values):
        wide = jnp.concatenate([tile, values], 1)
        return pltpu.roll(wide, 1, 1)[:, LANES:]

    def arrive(k):
        c = cols(wrap(py + k))
        for z in range(count_z):
            landed(main.at[band(z), c], main_r.at[k * count_z + z])
        forward(k, begin)

    def project(k):
        @pl.when(k + AHEAD < count_y)
        def _():
            pressure_sends(k + AHEAD, begin)

        @pl.when(k + AHEAD_F < count_y)
        def _():
            fluid_sends(k + AHEAD_F, begin)

        @pl.when(k + 1 < count_y)
        def _():
            arrive(k + 1)

        y = wrap(py + k)
        c = cols(y)
        for z in range(count_z):
            @pl.when(passed(pz, z) == 0)
            def _():
                landed(halo.at[band(z), c], halo_r.at[k * count_z + z])

            @pl.when(passed(pz, z) > 0)
            def _():
                landed(halo.at[band(z), c], fwd_r.at[k * count_z + z])

        @pl.when(me > 0)
        def _():
            landed(f_low.at[:, c], f_r.at[k])

        fluid = f[:, c]
        here = main[:, c]
        w_x = 0.5 * (fluid + f_low[:, c])
        along_x = w_x * (v[0, :, c] - (here - halo[:, c]))
        out[0, :, c] = jnp.where(me == 0, jnp.float32(0.0), along_x)
        lend(k, begin)
        z_index = lax.broadcasted_iota(jnp.int32, fluid.shape, 0)
        w_z = 0.5 * (fluid + pltpu.roll(fluid, 1, 0))
        along_z = w_z * (v[1, :, c] - (here - pltpu.roll(here, 1, 0)))
        out[1, :, c] = jnp.where(z_index == 0, jnp.float32(0.0), along_z)
        y_index = lax.broadcasted_iota(jnp.int32, fluid.shape, 1) + y * width
        f_tile = f[:, pl.ds(pl.multiple_of(wrap(y - 1) * width + (width - LANES), LANES), LANES)]
        w_y = 0.5 * (fluid + before(f_tile, fluid))
        along_y = w_y * (v[2, :, c] - (here - before(left[...], here)))
        out[2, :, c] = jnp.where(y_index == 0, jnp.float32(0.0), along_y)
        left[...] = here[:, width - LANES:]

    def diverge(k):
        y = wrap(py + k)
        c = cols(y)
        along_z = out[1, :, c]
        along_y = out[2, :, c]
        z_index = lax.broadcasted_iota(jnp.int32, along_z.shape, 0)
        y_index = lax.broadcasted_iota(jnp.int32, along_z.shape, 1) + y * width
        z_next = jnp.where(z_index == rows - 1, jnp.float32(0.0), pltpu.roll(along_z, rows - 1, 0))
        tile = out[2, :, pl.ds(pl.multiple_of(wrap(y + 1) * width, width), LANES)]
        wide = pltpu.roll(jnp.concatenate([along_y, tile], 1), width + LANES - 1, 1)[:, :width]
        y_next = jnp.where(y_index == across - 1, jnp.float32(0.0), wide)
        part[:, c] = (z_next - along_z) + (y_next - along_y) - out[0, :, c]

        for g in range(count_z):
            @pl.when(passed_up(pz, g) > 0)
            def _():
                landed(next_x.at[band(g), c], nx_r.at[k * count_z + g])
                part[band(g), c] = part[band(g), c] + next_x[band(g), c]

        result_sends(k, begin)

    def step(k, carry):
        @pl.when(k < count_y)
        def _():
            project(k)

        @pl.when(k > 0)
        def _():
            diverge(k - 1)
        return carry

    arrive(0)
    lax.fori_loop(0, count_y + 1, step, 0)

    def collect(i, carry):
        y = wrap(py - i - 1)
        for z in range(count_z):
            q = y * count_z + z
            landed(got.at[q], a_r.at[q])
            added = jnp.minimum(planes - 1 - q, 1 - passed_up(z, pz))

            @pl.when(added > 0)
            def _():
                landed(got_x.at[q], x_r.at[q])
                div[q] = got[q] + got_x[q]

            @pl.when(added <= 0)
            def _():
                div[q] = got[q]
        return carry

    lax.fori_loop(0, count_y, collect, 0)

    def finish(k, carry):
        pressure_sends(k, sent)
        fluid_sends(k, sent)
        forward(k, sent)
        lend(k, sent)
        result_sends(k, sent)
        return carry

    edge_sends(sent)
    lax.fori_loop(0, count_y, finish, 0)


def on_device(velocity, fluid, pressure):
    count_y = lax.axis_size("py")
    count_z = lax.axis_size("pz")
    rows, across = fluid.shape[1:]
    planes = pressure.shape[0]
    block = pressure.shape[1:]
    vm = lambda *shape: pltpu.VMEM(shape, jnp.float32)
    dma = lambda n: pltpu.SemaphoreType.DMA((n,))
    steps = count_y * count_z
    return pl.pallas_call(
        functools.partial(kernel, count_y, count_z),
        out_shape=(
            jax.ShapeDtypeStruct(velocity.shape, jnp.float32),
            jax.ShapeDtypeStruct(pressure.shape, jnp.float32),
        ),
        in_specs=[pl.BlockSpec(memory_space=pltpu.MemorySpace.HBM)] * 3,
        out_specs=(pl.BlockSpec(memory_space=pltpu.VMEM),) * 2,
        scratch_shapes=[
            vm(3, rows, across), vm(rows, across), vm(rows, across), vm(rows, across), vm(rows, across),
            vm(rows, LANES), vm(rows, across), vm(rows, across),
            vm(planes, *block), vm(planes, *block), dma(2),
            dma(steps), dma(steps), dma(steps), dma(steps), dma(count_z), dma(count_z),
            dma(count_y), dma(count_y), dma(steps), dma(steps), dma(steps), dma(steps),
            dma(steps), dma(planes), dma(steps), dma(planes),
        ],
        compiler_params=pltpu.CompilerParams(
            collective_id=0, has_side_effects=True, vmem_limit_bytes=40 << 20
        ),
        name="project_all",
    )(*(pltpu.with_memory_space_constraint(x, pltpu.MemorySpace.HBM) for x in (velocity, fluid, pressure)))


def solution(mesh):
    placed = (P(None, ("py", "pz"), None, None), P(("py", "pz"), None, None), P(None, "pz", "py"))
    return jax.shard_map(
        on_device,
        mesh=mesh,
        in_specs=placed,
        out_specs=(P(None, ("py", "pz"), None, None), P(None, "pz", "py")),
        check_vma=False,
    )
```

```python
import functools

import jax
import jax.numpy as jnp
from jax import lax
from jax.experimental import pallas as pl
from jax.experimental.pallas import tpu as pltpu
from jax.sharding import PartitionSpec as P

AHEAD = 3
AHEAD_F = 1
LAG = 3
LANES = 128


def clip(n):
    return min(max(n, 0), 1) if isinstance(n, int) else jnp.minimum(jnp.maximum(n, 0), 1)


def kernel(
    count_y, count_z, v_hbm, f_hbm, p_hbm, out_ref, div,
    v, f, f_low, press, result, next_x, got,
    in_sem, main_s, main_r, halo_r, lift_s, drop_s, f_s, f_r, nx_s, nx_r, a_s, a_r,
):
    out = out_ref.at[:, 0]
    py = lax.axis_index("py")
    pz = lax.axis_index("pz")
    me = py * count_z + pz
    planes = count_y * count_z
    last = count_z - 1
    rows, across = f.shape
    width = across // count_y
    part_rows = rows // count_z
    half = count_z // 2 if count_z % 2 == 0 else 1
    inner = clip(me)

    def side(z):
        return z // half if isinstance(z, int) else lax.div(z, half)

    def joined(z):
        return min((z + 1) % half, 1) if isinstance(z, int) else jnp.minimum(lax.rem(z + 1, half), 1)

    def cols(c):
        return pl.ds(pl.multiple_of(c * width, width), width)

    def band(g):
        return pl.ds(g * part_rows, part_rows)

    def wrap(c):
        return lax.rem(c + 2 * count_y, count_y)

    def remote(src, dst, send, recv, y, z):
        return pltpu.make_async_remote_copy(
            src_ref=src, dst_ref=dst, send_sem=send, recv_sem=recv,
            device_id=(y, z), device_id_type=pl.DeviceIdType.MESH,
        )

    def begin(src, dst, send, recv, y, z, gate=1, away=False):
        apart = 1 if away else clip(jnp.abs(y * count_z + z - me))

        @pl.when(apart * gate > 0)
        def _():
            remote(src, dst, send, recv, y, z).start()

        if not away:
            @pl.when((1 - apart) * gate > 0)
            def _():
                pltpu.make_async_copy(src, dst, recv).start()

    def sent(src, dst, send, recv, y, z, gate=1, away=False):
        apart = 1 if away else clip(jnp.abs(y * count_z + z - me))

        @pl.when(apart * gate > 0)
        def _():
            remote(src, dst, send, recv, y, z).wait_send()

    def landed(dst, recv, gate=None):
        if gate is None:
            pltpu.make_async_copy(dst, dst, recv).wait()
        else:
            @pl.when(gate > 0)
            def _():
                pltpu.make_async_copy(dst, dst, recv).wait()

    def passed(z, g):
        low, high = (min, max) if isinstance(z, int) and isinstance(g, int) else (jnp.minimum, jnp.maximum)
        apart = low(high(abs(g - z) - 1, 0), 1)
        across_middle = joined(z - 1) * low(abs(side(g) - side(z)), 1)
        return low(high(apart, across_middle), low(z, 1))

    def passed_up(z, g):
        return passed(z + 1, g) if isinstance(z, int) and z < count_z - 1 else (
            0 if isinstance(z, int) else jnp.minimum(passed(z + 1, g), count_z - 1 - z))

    loads = [
        pltpu.make_async_copy(v_hbm.at[:, 0], v, in_sem.at[0]),
        pltpu.make_async_copy(f_hbm.at[0], f, in_sem.at[1]),
    ]
    for load in loads:
        load.start()

    barrier = pltpu.get_barrier_semaphore()

    def greet(i, carry):
        @pl.when(i != me)
        def _():
            pl.semaphore_signal(
                barrier, inc=1, device_id=(lax.div(i, count_z), lax.rem(i, count_z)),
                device_id_type=pl.DeviceIdType.MESH,
            )
        return carry

    lax.fori_loop(0, planes, greet, 0)
    pl.semaphore_wait(barrier, planes - 1)

    mine = pl.ds(pl.multiple_of(pz * part_rows, part_rows), part_rows)
    ahead_y = lax.div(me + 1, count_z)
    ahead_z = lax.rem(me + 1, count_z)

    def main_direct(z, g):
        return 1 if isinstance(z, int) and z == last else jnp.maximum(clip(z + 2 - g), clip(z - last + 1))

    def halo_direct(z, g):
        return 1 if isinstance(z, int) and z == 0 else jnp.maximum(clip(g - z + 2), clip(1 - z))

    def lifts(g):
        return clip(last - pz) * clip(pz - g)

    def drops(g):
        return clip(pz) * clip(g - pz)

    def pair(g):
        return inner * main_direct(pz, g) * halo_direct(pz, g)

    def turn(j):
        return wrap(j - 1)

    def pressure_sends(j, do):
        k = turn(j)
        y = wrap(py - k)
        for z in range(count_z):
            target = y * count_z + z
            slot = k * count_z + z
            at = k * count_z + pz
            m, h = main_direct(z, pz), halo_direct(z, pz) * clip(target)
            do(p_hbm.at[pl.ds(jnp.maximum(target - 1, 0), 2)], press.at[:, mine, cols(py)], main_s.at[slot], main_r.at[at], y, z, gate=m * h)
            do(p_hbm.at[target], press.at[1, mine, cols(py)], main_s.at[slot], main_r.at[at], y, z, gate=m * (1 - h))
            do(p_hbm.at[jnp.maximum(target - 1, 0)], press.at[0, mine, cols(py)], main_s.at[slot], halo_r.at[at], y, z, gate=h * (1 - m))

    def fluid_sends(k, do):
        c = cols(wrap(ahead_y + k))
        do(f_hbm.at[0, :, c], f_low.at[:, c], f_s.at[k], f_r.at[k], ahead_y, ahead_z,
           gate=clip(planes - 1 - me), away=True)

    def lift(k, g, do):
        c = cols(wrap(py + k))
        slot = k * count_z + g
        do(press.at[1, band(g), c], press.at[0, band(g), c], lift_s.at[slot], halo_r.at[slot], py, pz + 1,
           gate=lifts(g), away=True)

    def drop(k, g, do):
        c = cols(wrap(py + k))
        slot = k * count_z + g
        do(press.at[0, band(g), c], press.at[1, band(g), c], drop_s.at[slot], main_r.at[slot], py, pz - 1,
           gate=drops(g), away=True)

    def arrive(j):
        k = turn(j)
        c = cols(wrap(py + k))
        for g in range(count_z):
            slot = k * count_z + g
            up, down, two = lifts(g), drops(g), pair(g)
            landed(press.at[:, band(g), c], main_r.at[slot], (up + down) * two)
            landed(press.at[1, band(g), c], main_r.at[slot], up * (1 - two))
            landed(press.at[0, band(g), c], halo_r.at[slot], down * (1 - two))
            lift(k, g, begin)
            drop(k, g, begin)

    def ready(j):
        k = turn(j)
        c = cols(wrap(py + k))
        for g in range(count_z):
            slot = k * count_z + g
            up, down, two = lifts(g), drops(g), pair(g)
            landed(press.at[:, band(g), c], main_r.at[slot], (1 - up - down) * two)
            landed(press.at[1, band(g), c], main_r.at[slot], (1 - up) * (1 - two))
            landed(press.at[0, band(g), c], halo_r.at[slot], (1 - down) * (1 - two) * inner)

    def lend(k, do):
        c = cols(wrap(py + k))
        for g in range(count_z):
            slot = k * count_z + g
            do(result.at[0, band(g), c], next_x.at[band(g), c], nx_s.at[slot], nx_r.at[slot], py, pz - 1,
               gate=passed(pz, g), away=True)

    def result_sends(k, do):
        y = wrap(py + k)
        for z in range(count_z):
            slot = k * count_z + z
            two = inner * (1 - passed(pz, z))
            do(result.at[:, band(z), cols(y)], got.at[me], a_s.at[slot], a_r.at[me], y, z, gate=two)
            do(result.at[1, band(z), cols(y)], got.at[me, 1], a_s.at[slot], a_r.at[me], y, z, gate=1 - two)

    for j in range(min(AHEAD, count_y)):
        pressure_sends(j, begin)
    for k in range(min(AHEAD_F, count_y)):
        fluid_sends(k, begin)
    for load in loads:
        load.wait()

    def tile_at(c):
        return pl.ds(pl.multiple_of(c * width + (width - LANES), LANES), LANES)

    def before(tile, values):
        wide = jnp.concatenate([tile, values], 1)
        return pltpu.roll(wide, 1, 1)[:, LANES:]

    def project(k):
        y = wrap(py + k)
        c = cols(y)

        @pl.when(me > 0)
        def _():
            landed(f_low.at[:, c], f_r.at[k])

        fluid = f[:, c]
        here = press[1, :, c]
        w_x = 0.5 * (fluid + f_low[:, c])
        along_x = w_x * (v[0, :, c] - (here - press[0, :, c]))
        along_x = jnp.where(me == 0, jnp.float32(0.0), along_x)
        out[0, :, c] = along_x
        result[0, :, c] = along_x
        lend(k, begin)
        z_index = lax.broadcasted_iota(jnp.int32, fluid.shape, 0)
        w_z = 0.5 * (fluid + pltpu.roll(fluid, 1, 0))
        along_z = w_z * (v[1, :, c] - (here - pltpu.roll(here, 1, 0)))
        out[1, :, c] = jnp.where(z_index == 0, jnp.float32(0.0), along_z)
        y_index = lax.broadcasted_iota(jnp.int32, fluid.shape, 1) + y * width
        tile = tile_at(wrap(y - 1))
        w_y = 0.5 * (fluid + before(f[:, tile], fluid))
        along_y = w_y * (v[2, :, c] - (here - before(press[1, :, tile], here)))
        out[2, :, c] = jnp.where(y_index == 0, jnp.float32(0.0), along_y)

    def diverge(k):
        y = wrap(py + k)
        c = cols(y)
        along_z = out[1, :, c]
        along_y = out[2, :, c]
        z_index = lax.broadcasted_iota(jnp.int32, along_z.shape, 0)
        y_index = lax.broadcasted_iota(jnp.int32, along_z.shape, 1) + y * width
        z_next = jnp.where(z_index == rows - 1, jnp.float32(0.0), pltpu.roll(along_z, rows - 1, 0))
        tile = out[2, :, pl.ds(pl.multiple_of(wrap(y + 1) * width, width), LANES)]
        wide = pltpu.roll(jnp.concatenate([along_y, tile], 1), width + LANES - 1, 1)[:, :width]
        y_next = jnp.where(y_index == across - 1, jnp.float32(0.0), wide)
        result[1, :, c] = (z_next - along_z) + (y_next - along_y) - out[0, :, c]

        for g in range(count_z):
            @pl.when(passed_up(pz, g) > 0)
            def _():
                landed(next_x.at[band(g), c], nx_r.at[k * count_z + g])
                result[1, band(g), c] = result[1, band(g), c] + next_x[band(g), c]

        result_sends(k, begin)

    def store(q, z):
        added = clip(planes - 1 - q) * (1 - passed_up(z, pz))

        @pl.when(added > 0)
        def _():
            div[q] = got[q, 1] + got[jnp.minimum(q + 1, planes - 1), 0]

        @pl.when(added <= 0)
        def _():
            div[q] = got[q, 1]

    def collect(k):
        y = wrap(py - k)
        for z in range(count_z):
            q = y * count_z + z
            two = clip(q) * (1 - passed(z, pz))
            landed(got.at[q], a_r.at[q], two)
            landed(got.at[q, 1], a_r.at[q], 1 - two)
        for z in range(last):
            store(y * count_z + z, z)

        @pl.when(k > 0)
        def _():
            store(y * count_z + last, last)

    arrive(0)
    ready(0)
    if count_y > 1:
        arrive(1)

    def step(k, carry):
        @pl.when(k + AHEAD < count_y)
        def _():
            pressure_sends(k + AHEAD, begin)

        @pl.when(k + AHEAD_F < count_y)
        def _():
            fluid_sends(k + AHEAD_F, begin)

        @pl.when(k + 2 < count_y)
        def _():
            arrive(k + 2)

        @pl.when(k + 1 < count_y)
        def _():
            ready(k + 1)

        @pl.when(k < count_y)
        def _():
            project(k)

        @pl.when(k > 0)
        def _():
            diverge(k - 1)

        @pl.when(k >= LAG)
        def _():
            collect(k - LAG)
        return carry

    lax.fori_loop(0, count_y + 1, step, 0)

    def finish(k, carry):
        pressure_sends(k, sent)
        fluid_sends(k, sent)
        for g in range(count_z):
            lift(k, g, sent)
            drop(k, g, sent)
        lend(k, sent)
        result_sends(k, sent)
        return carry

    lax.fori_loop(0, count_y, finish, 0)

    def rest(k, carry):
        collect(k)
        return carry

    lax.fori_loop(max(count_y + 1 - LAG, 0), count_y, rest, 0)
    store(me - pz + last, last)


def on_device(velocity, fluid, pressure):
    count_y = lax.axis_size("py")
    count_z = lax.axis_size("pz")
    rows, across = fluid.shape[1:]
    planes = pressure.shape[0]
    block = pressure.shape[1:]
    vm = lambda *shape: pltpu.VMEM(shape, jnp.float32)
    dma = lambda n: pltpu.SemaphoreType.DMA((n,))
    steps = count_y * count_z
    return pl.pallas_call(
        functools.partial(kernel, count_y, count_z),
        out_shape=(
            jax.ShapeDtypeStruct(velocity.shape, jnp.float32),
            jax.ShapeDtypeStruct(pressure.shape, jnp.float32),
        ),
        in_specs=[pl.BlockSpec(memory_space=pltpu.MemorySpace.HBM)] * 3,
        out_specs=(pl.BlockSpec(memory_space=pltpu.VMEM),) * 2,
        scratch_shapes=[
            vm(3, rows, across), vm(rows, across), vm(rows, across), vm(2, rows, across), vm(2, rows, across),
            vm(rows, across), vm(planes, 2, *block), dma(2),
            dma(steps), dma(steps), dma(steps), dma(steps), dma(steps),
            dma(count_y), dma(count_y), dma(steps), dma(steps), dma(steps), dma(planes),
        ],
        compiler_params=pltpu.CompilerParams(
            collective_id=0, has_side_effects=True, vmem_limit_bytes=40 << 20
        ),
        name="project_all",
    )(*(pltpu.with_memory_space_constraint(x, pltpu.MemorySpace.HBM) for x in (velocity, fluid, pressure)))


def solution(mesh):
    placed = (P(None, ("py", "pz"), None, None), P(("py", "pz"), None, None), P(None, "pz", "py"))
    return jax.shard_map(
        on_device,
        mesh=mesh,
        in_specs=placed,
        out_specs=(P(None, ("py", "pz"), None, None), P(None, "pz", "py")),
        check_vma=False,
    )
```

```python
import functools

import jax
import jax.numpy as jnp
from jax import lax
from jax.experimental import pallas as pl
from jax.experimental.pallas import tpu as pltpu
from jax.sharding import PartitionSpec as P

AHEAD = 3
AHEAD_F = 3
LAG = 3
LANES = 128
PIECES = 1


def clip(n):
    return min(max(n, 0), 1) if isinstance(n, int) else jnp.minimum(jnp.maximum(n, 0), 1)


def kernel(
    count_y, count_z, v_hbm, f_hbm, p_hbm, out_ref, div,
    v, f, f_low, press, result, next_x, got,
    in_sem, main_s, main_r, halo_r, lift_s, drop_s, f_s, f_r, nx_s, nx_r, a_s, a_r,
):
    out = out_ref.at[:, 0]
    py = lax.axis_index("py")
    pz = lax.axis_index("pz")
    me = py * count_z + pz
    planes = count_y * count_z
    last = count_z - 1
    rows, across = f.shape
    width = across // count_y
    part_rows = rows // count_z
    half = count_z // 2 if count_z % 2 == 0 else 1
    inner = clip(me)

    def side(z):
        return z // half if isinstance(z, int) else lax.div(z, half)

    def joined(z):
        return min((z + 1) % half, 1) if isinstance(z, int) else jnp.minimum(lax.rem(z + 1, half), 1)

    def cols(c):
        return pl.ds(pl.multiple_of(c * width, width), width)

    def band(g):
        return pl.ds(g * part_rows, part_rows)

    def wrap(c):
        return lax.rem(c + 2 * count_y, count_y)

    def remote(src, dst, send, recv, y, z):
        return pltpu.make_async_remote_copy(
            src_ref=src, dst_ref=dst, send_sem=send, recv_sem=recv,
            device_id=(y, z), device_id_type=pl.DeviceIdType.MESH,
        )

    def begin(src, dst, send, recv, y, z, gate=1, away=False):
        apart = 1 if away else clip(jnp.abs(y * count_z + z - me))

        @pl.when(apart * gate > 0)
        def _():
            remote(src, dst, send, recv, y, z).start()

        if not away:
            @pl.when((1 - apart) * gate > 0)
            def _():
                pltpu.make_async_copy(src, dst, recv).start()

    def sent(src, dst, send, recv, y, z, gate=1, away=False):
        apart = 1 if away else clip(jnp.abs(y * count_z + z - me))

        @pl.when(apart * gate > 0)
        def _():
            remote(src, dst, send, recv, y, z).wait_send()

    def landed(dst, recv, gate=None):
        if gate is None:
            pltpu.make_async_copy(dst, dst, recv).wait()
        else:
            @pl.when(gate > 0)
            def _():
                pltpu.make_async_copy(dst, dst, recv).wait()

    def passed(z, g):
        low, high = (min, max) if isinstance(z, int) and isinstance(g, int) else (jnp.minimum, jnp.maximum)
        apart = low(high(abs(g - z) - 1, 0), 1)
        across_middle = joined(z - 1) * low(abs(side(g) - side(z)), 1)
        return low(high(apart, across_middle), low(z, 1))

    def passed_up(z, g):
        return passed(z + 1, g) if isinstance(z, int) and z < count_z - 1 else (
            0 if isinstance(z, int) else jnp.minimum(passed(z + 1, g), count_z - 1 - z))

    loads = [
        pltpu.make_async_copy(v_hbm.at[:, 0], v, in_sem.at[0]),
        pltpu.make_async_copy(f_hbm.at[0], f, in_sem.at[1]),
    ]
    for load in loads:
        load.start()

    barrier = pltpu.get_barrier_semaphore()

    def greet(i, carry):
        @pl.when(i != me)
        def _():
            pl.semaphore_signal(
                barrier, inc=1, device_id=(lax.div(i, count_z), lax.rem(i, count_z)),
                device_id_type=pl.DeviceIdType.MESH,
            )
        return carry

    lax.fori_loop(0, planes, greet, 0)
    pl.semaphore_wait(barrier, planes - 1)

    mine = pl.ds(pl.multiple_of(pz * part_rows, part_rows), part_rows)
    ahead_y = lax.div(me + 1, count_z)
    ahead_z = lax.rem(me + 1, count_z)

    def main_direct(z, g):
        return 1 if isinstance(z, int) and z == last else jnp.maximum(clip(z + 2 - g), clip(z - last + 1))

    def halo_direct(z, g):
        return 1 if isinstance(z, int) and z == 0 else jnp.maximum(clip(g - z + 2), clip(1 - z))

    def lifts(g):
        return clip(last - pz) * clip(pz - g)

    def drops(g):
        return clip(pz) * clip(g - pz)

    def pair(g):
        return inner * main_direct(pz, g) * halo_direct(pz, g)

    def turn(j):
        return wrap(j - 1)

    def pressure_sends(j, do):
        k = turn(j)
        y = wrap(py - k)
        for z in range(count_z):
            target = y * count_z + z
            slot = k * count_z + z
            at = k * count_z + pz
            m, h = main_direct(z, pz), halo_direct(z, pz) * clip(target)
            do(p_hbm.at[pl.ds(jnp.maximum(target - 1, 0), 2)], press.at[:, mine, cols(py)], main_s.at[slot], main_r.at[at], y, z, gate=m * h)
            do(p_hbm.at[target], press.at[1, mine, cols(py)], main_s.at[slot], main_r.at[at], y, z, gate=m * (1 - h))
            do(p_hbm.at[jnp.maximum(target - 1, 0)], press.at[0, mine, cols(py)], main_s.at[slot], halo_r.at[at], y, z, gate=h * (1 - m))

    def fluid_sends(k, do):
        c = cols(wrap(ahead_y + k))
        do(f_hbm.at[0, :, c], f_low.at[:, c], f_s.at[k], f_r.at[k], ahead_y, ahead_z,
           gate=clip(planes - 1 - me), away=True)

    def lift(k, g, do):
        c = cols(wrap(py + k))
        slot = k * count_z + g
        do(press.at[1, band(g), c], press.at[0, band(g), c], lift_s.at[slot], halo_r.at[slot], py, pz + 1,
           gate=lifts(g), away=True)

    def drop(k, g, do):
        c = cols(wrap(py + k))
        slot = k * count_z + g
        do(press.at[0, band(g), c], press.at[1, band(g), c], drop_s.at[slot], main_r.at[slot], py, pz - 1,
           gate=drops(g), away=True)

    def arrive(j):
        k = turn(j)
        c = cols(wrap(py + k))
        for g in range(count_z):
            slot = k * count_z + g
            up, down, two = lifts(g), drops(g), pair(g)
            landed(press.at[:, band(g), c], main_r.at[slot], (up + down) * two)
            landed(press.at[1, band(g), c], main_r.at[slot], up * (1 - two))
            landed(press.at[0, band(g), c], halo_r.at[slot], down * (1 - two))
            lift(k, g, begin)
            drop(k, g, begin)

    def ready(j):
        k = turn(j)
        c = cols(wrap(py + k))
        for g in range(count_z):
            slot = k * count_z + g
            up, down, two = lifts(g), drops(g), pair(g)
            landed(press.at[:, band(g), c], main_r.at[slot], (1 - up - down) * two)
            landed(press.at[1, band(g), c], main_r.at[slot], (1 - up) * (1 - two))
            landed(press.at[0, band(g), c], halo_r.at[slot], (1 - down) * (1 - two) * inner)

    def lend(k, do):
        c = cols(wrap(py + k))
        for g in range(count_z):
            slot = k * count_z + g
            do(result.at[0, band(g), c], next_x.at[band(g), c], nx_s.at[slot], nx_r.at[slot], py, pz - 1,
               gate=passed(pz, g), away=True)

    def result_sends(k, do):
        y = wrap(py + k)
        for z in range(count_z):
            slot = k * count_z + z
            two = inner * (1 - passed(pz, z))
            do(result.at[:, band(z), cols(y)], got.at[me], a_s.at[slot], a_r.at[me], y, z, gate=two)
            do(result.at[1, band(z), cols(y)], got.at[me, 1], a_s.at[slot], a_r.at[me], y, z, gate=1 - two)

    for j in range(min(AHEAD, count_y)):
        pressure_sends(j, begin)
    for k in range(min(AHEAD_F, count_y)):
        fluid_sends(k, begin)
    for load in loads:
        load.wait()

    def tile_at(c):
        return pl.ds(pl.multiple_of(c * width + (width - LANES), LANES), LANES)

    def before(tile, values):
        wide = jnp.concatenate([tile, values], 1)
        return pltpu.roll(wide, 1, 1)[:, LANES:]

    def project(k):
        y = wrap(py + k)
        c = cols(y)

        @pl.when(me > 0)
        def _():
            landed(f_low.at[:, c], f_r.at[k])

        fluid = f[:, c]
        here = press[1, :, c]
        w_x = 0.5 * (fluid + f_low[:, c])
        along_x = w_x * (v[0, :, c] - (here - press[0, :, c]))
        along_x = jnp.where(me == 0, jnp.float32(0.0), along_x)
        out[0, :, c] = along_x
        result[0, :, c] = along_x
        lend(k, begin)
        z_index = lax.broadcasted_iota(jnp.int32, fluid.shape, 0)
        w_z = 0.5 * (fluid + pltpu.roll(fluid, 1, 0))
        along_z = w_z * (v[1, :, c] - (here - pltpu.roll(here, 1, 0)))
        out[1, :, c] = jnp.where(z_index == 0, jnp.float32(0.0), along_z)
        y_index = lax.broadcasted_iota(jnp.int32, fluid.shape, 1) + y * width
        tile = tile_at(wrap(y - 1))
        w_y = 0.5 * (fluid + before(f[:, tile], fluid))
        along_y = w_y * (v[2, :, c] - (here - before(press[1, :, tile], here)))
        out[2, :, c] = jnp.where(y_index == 0, jnp.float32(0.0), along_y)

    def diverge(k):
        y = wrap(py + k)
        c = cols(y)
        along_z = out[1, :, c]
        along_y = out[2, :, c]
        z_index = lax.broadcasted_iota(jnp.int32, along_z.shape, 0)
        y_index = lax.broadcasted_iota(jnp.int32, along_z.shape, 1) + y * width
        z_next = jnp.where(z_index == rows - 1, jnp.float32(0.0), pltpu.roll(along_z, rows - 1, 0))
        tile = out[2, :, pl.ds(pl.multiple_of(wrap(y + 1) * width, width), LANES)]
        wide = pltpu.roll(jnp.concatenate([along_y, tile], 1), width + LANES - 1, 1)[:, :width]
        y_next = jnp.where(y_index == across - 1, jnp.float32(0.0), wide)
        result[1, :, c] = (z_next - along_z) + (y_next - along_y) - out[0, :, c]

        for g in range(count_z):
            @pl.when(passed_up(pz, g) > 0)
            def _():
                landed(next_x.at[band(g), c], nx_r.at[k * count_z + g])
                result[1, band(g), c] = result[1, band(g), c] + next_x[band(g), c]

        result_sends(k, begin)

    def store(q, z):
        added = clip(planes - 1 - q) * (1 - passed_up(z, pz))

        @pl.when(added > 0)
        def _():
            div[q] = got[q, 1] + got[jnp.minimum(q + 1, planes - 1), 0]

        @pl.when(added <= 0)
        def _():
            div[q] = got[q, 1]

    def collect(k):
        y = wrap(py - k)
        for z in range(count_z):
            q = y * count_z + z
            two = clip(q) * (1 - passed(z, pz))
            landed(got.at[q], a_r.at[q], two)
            landed(got.at[q, 1], a_r.at[q], 1 - two)
        for z in range(last):
            store(y * count_z + z, z)

        @pl.when(k > 0)
        def _():
            store(y * count_z + last, last)

    arrive(0)
    ready(0)
    if count_y > 1:
        arrive(1)

    def step(k, carry):
        @pl.when(k + AHEAD < count_y)
        def _():
            pressure_sends(k + AHEAD, begin)

        @pl.when(k + AHEAD_F < count_y)
        def _():
            fluid_sends(k + AHEAD_F, begin)

        @pl.when(k + 2 < count_y)
        def _():
            arrive(k + 2)

        @pl.when(k + 1 < count_y)
        def _():
            ready(k + 1)

        @pl.when(k < count_y)
        def _():
            project(k)

        @pl.when(k > 0)
        def _():
            diverge(k - 1)

        @pl.when(k >= LAG)
        def _():
            collect(k - LAG)
        return carry

    lax.fori_loop(0, count_y + 1, step, 0)

    def finish(k, carry):
        pressure_sends(k, sent)
        fluid_sends(k, sent)
        for g in range(count_z):
            lift(k, g, sent)
            drop(k, g, sent)
        lend(k, sent)
        result_sends(k, sent)
        return carry

    lax.fori_loop(0, count_y, finish, 0)

    def rest(k, carry):
        collect(k)
        return carry

    lax.fori_loop(max(count_y + 1 - LAG, 0), count_y, rest, 0)
    store(me - pz + last, last)


def write_out(updated, total, updated_hbm, total_hbm, sem):
    rows, planes = updated.shape[2] // PIECES, total.shape[0] // PIECES
    copies = []
    for i in range(PIECES):
        for d in range(3):
            part = (d, 0, pl.ds(i * rows, rows))
            copies.append(pltpu.make_async_copy(updated.at[part], updated_hbm.at[part], sem.at[len(copies)]))
        part = pl.ds(i * planes, planes)
        copies.append(pltpu.make_async_copy(total.at[part], total_hbm.at[part], sem.at[len(copies)]))
    for copy in copies:
        copy.start()
    for copy in copies:
        copy.wait()


def on_device(velocity, fluid, pressure):
    count_y = lax.axis_size("py")
    count_z = lax.axis_size("pz")
    rows, across = fluid.shape[1:]
    planes = pressure.shape[0]
    block = pressure.shape[1:]
    vm = lambda *shape: pltpu.VMEM(shape, jnp.float32)
    dma = lambda n: pltpu.SemaphoreType.DMA((n,))
    steps = count_y * count_z
    updated, total = pl.pallas_call(
        functools.partial(kernel, count_y, count_z),
        out_shape=(
            jax.ShapeDtypeStruct(velocity.shape, jnp.float32),
            jax.ShapeDtypeStruct(pressure.shape, jnp.float32),
        ),
        in_specs=[pl.BlockSpec(memory_space=pltpu.MemorySpace.HBM)] * 3,
        out_specs=(pl.BlockSpec(memory_space=pltpu.VMEM),) * 2,
        scratch_shapes=[
            vm(3, rows, across), vm(rows, across), vm(rows, across), vm(2, rows, across), vm(2, rows, across),
            vm(rows, across), vm(planes, 2, *block), dma(2),
            dma(steps), dma(steps), dma(steps), dma(steps), dma(steps),
            dma(count_y), dma(count_y), dma(steps), dma(steps), dma(steps), dma(planes),
        ],
        compiler_params=pltpu.CompilerParams(
            collective_id=0, has_side_effects=True, vmem_limit_bytes=40 << 20
        ),
        name="project_all",
    )(*(pltpu.with_memory_space_constraint(x, pltpu.MemorySpace.HBM) for x in (velocity, fluid, pressure)))
    return pl.pallas_call(
        write_out,
        out_shape=(
            jax.ShapeDtypeStruct(velocity.shape, jnp.float32),
            jax.ShapeDtypeStruct(pressure.shape, jnp.float32),
        ),
        in_specs=[pl.BlockSpec(memory_space=pltpu.VMEM)] * 2,
        out_specs=(pl.BlockSpec(memory_space=pltpu.MemorySpace.HBM),) * 2,
        scratch_shapes=[dma(PIECES * 4)],
        compiler_params=pltpu.CompilerParams(vmem_limit_bytes=40 << 20),
        name="write_out",
    )(updated, total)


def solution(mesh):
    placed = (P(None, ("py", "pz"), None, None), P(("py", "pz"), None, None), P(None, "pz", "py"))
    return jax.shard_map(
        on_device,
        mesh=mesh,
        in_specs=placed,
        out_specs=(P(None, ("py", "pz"), None, None), P(None, "pz", "py")),
        check_vma=False,
    )
```

```python
import functools

import jax
import jax.numpy as jnp
from jax import lax
from jax.experimental import pallas as pl
from jax.experimental.pallas import tpu as pltpu
from jax.sharding import PartitionSpec as P

AHEAD = 3
AHEAD_F = 4
LATE = 3
LAG = 5
LANES = 128
PIECES = 1


def clip(n):
    return min(max(n, 0), 1) if isinstance(n, int) else jnp.minimum(jnp.maximum(n, 0), 1)


def kernel(
    count_y, count_z, v_hbm, f_hbm, p_hbm, out_ref, div,
    v, f, f_low, press, result, next_x, got,
    in_sem, main_s, main_r, halo_r, lift_s, drop_s, f_s, f_r, nx_s, nx_r, a_s, a_r,
):
    out = out_ref.at[:, 0]
    py = lax.axis_index("py")
    pz = lax.axis_index("pz")
    me = py * count_z + pz
    planes = count_y * count_z
    last = count_z - 1
    rows, across = f.shape
    width = across // count_y
    part_rows = rows // count_z
    half = count_z // 2 if count_z % 2 == 0 else 1
    inner = clip(me)

    def side(z):
        return z // half if isinstance(z, int) else lax.div(z, half)

    def joined(z):
        return min((z + 1) % half, 1) if isinstance(z, int) else jnp.minimum(lax.rem(z + 1, half), 1)

    def cols(c):
        return pl.ds(pl.multiple_of(c * width, width), width)

    def band(g):
        return pl.ds(g * part_rows, part_rows)

    def wrap(c):
        return lax.rem(c + 2 * count_y, count_y)

    def remote(src, dst, send, recv, y, z):
        return pltpu.make_async_remote_copy(
            src_ref=src, dst_ref=dst, send_sem=send, recv_sem=recv,
            device_id=(y, z), device_id_type=pl.DeviceIdType.MESH,
        )

    def begin(src, dst, send, recv, y, z, gate=1, away=False):
        apart = 1 if away else clip(jnp.abs(y * count_z + z - me))

        @pl.when(apart * gate > 0)
        def _():
            remote(src, dst, send, recv, y, z).start()

        if not away:
            @pl.when((1 - apart) * gate > 0)
            def _():
                pltpu.make_async_copy(src, dst, recv).start()

    def sent(src, dst, send, recv, y, z, gate=1, away=False):
        apart = 1 if away else clip(jnp.abs(y * count_z + z - me))

        @pl.when(apart * gate > 0)
        def _():
            remote(src, dst, send, recv, y, z).wait_send()

    def landed(dst, recv, gate=None):
        if gate is None:
            pltpu.make_async_copy(dst, dst, recv).wait()
        else:
            @pl.when(gate > 0)
            def _():
                pltpu.make_async_copy(dst, dst, recv).wait()

    def passed(z, g):
        low, high = (min, max) if isinstance(z, int) and isinstance(g, int) else (jnp.minimum, jnp.maximum)
        apart = low(high(abs(g - z) - 1, 0), 1)
        across_middle = joined(z - 1) * low(abs(side(g) - side(z)), 1)
        return low(high(apart, across_middle), low(z, 1))

    def passed_up(z, g):
        return passed(z + 1, g) if isinstance(z, int) and z < count_z - 1 else (
            0 if isinstance(z, int) else jnp.minimum(passed(z + 1, g), count_z - 1 - z))

    loads = [
        pltpu.make_async_copy(v_hbm.at[:, 0], v, in_sem.at[0]),
        pltpu.make_async_copy(f_hbm.at[0], f, in_sem.at[1]),
    ]
    for load in loads:
        load.start()

    barrier = pltpu.get_barrier_semaphore()

    def greet(i, carry):
        @pl.when(i != me)
        def _():
            pl.semaphore_signal(
                barrier, inc=1, device_id=(lax.div(i, count_z), lax.rem(i, count_z)),
                device_id_type=pl.DeviceIdType.MESH,
            )
        return carry

    lax.fori_loop(0, planes, greet, 0)
    pl.semaphore_wait(barrier, planes - 1)

    mine = pl.ds(pl.multiple_of(pz * part_rows, part_rows), part_rows)
    ahead_y = lax.div(me + 1, count_z)
    ahead_z = lax.rem(me + 1, count_z)

    def main_direct(z, g):
        return 1 if isinstance(z, int) and z == last else jnp.maximum(clip(z + 2 - g), clip(z - last + 1))

    def halo_direct(z, g):
        return 1 if isinstance(z, int) and z == 0 else jnp.maximum(clip(g - z + 2), clip(1 - z))

    def lifts(g):
        return clip(last - pz) * clip(pz - g)

    def drops(g):
        return clip(pz) * clip(g - pz)

    def pair(g):
        return inner * main_direct(pz, g) * halo_direct(pz, g)

    def turn(j):
        return wrap(j - 1)

    def pressure_sends(j, do):
        k = turn(j)
        y = wrap(py - k)
        for z in range(count_z):
            target = y * count_z + z
            slot = k * count_z + z
            at = k * count_z + pz
            m, h = main_direct(z, pz), halo_direct(z, pz) * clip(target)
            do(p_hbm.at[pl.ds(jnp.maximum(target - 1, 0), 2)], press.at[:, mine, cols(py)], main_s.at[slot], main_r.at[at], y, z, gate=m * h)
            do(p_hbm.at[target], press.at[1, mine, cols(py)], main_s.at[slot], main_r.at[at], y, z, gate=m * (1 - h))
            do(p_hbm.at[jnp.maximum(target - 1, 0)], press.at[0, mine, cols(py)], main_s.at[slot], halo_r.at[at], y, z, gate=h * (1 - m))

    def fluid_sends(k, do):
        c = cols(wrap(ahead_y + k))
        do(f_hbm.at[0, :, c], f_low.at[:, c], f_s.at[k], f_r.at[k], ahead_y, ahead_z,
           gate=clip(planes - 1 - me), away=True)

    def lift(k, g, do):
        c = cols(wrap(py + k))
        slot = k * count_z + g
        do(press.at[1, band(g), c], press.at[0, band(g), c], lift_s.at[slot], halo_r.at[slot], py, pz + 1,
           gate=lifts(g), away=True)

    def drop(k, g, do):
        c = cols(wrap(py + k))
        slot = k * count_z + g
        do(press.at[0, band(g), c], press.at[1, band(g), c], drop_s.at[slot], main_r.at[slot], py, pz - 1,
           gate=drops(g), away=True)

    def arrive(j):
        k = turn(j)
        c = cols(wrap(py + k))
        for g in range(count_z):
            slot = k * count_z + g
            up, down, two = lifts(g), drops(g), pair(g)
            landed(press.at[:, band(g), c], main_r.at[slot], (up + down) * two)
            landed(press.at[1, band(g), c], main_r.at[slot], up * (1 - two))
            landed(press.at[0, band(g), c], halo_r.at[slot], down * (1 - two))
            lift(k, g, begin)
            drop(k, g, begin)

    def ready(j):
        k = turn(j)
        c = cols(wrap(py + k))
        for g in range(count_z):
            slot = k * count_z + g
            up, down, two = lifts(g), drops(g), pair(g)
            landed(press.at[:, band(g), c], main_r.at[slot], (1 - up - down) * two)
            landed(press.at[1, band(g), c], main_r.at[slot], (1 - up) * (1 - two))
            landed(press.at[0, band(g), c], halo_r.at[slot], (1 - down) * (1 - two) * inner)

    def lend(k, do):
        c = cols(wrap(py + k))
        for g in range(count_z):
            slot = k * count_z + g
            do(result.at[0, band(g), c], next_x.at[band(g), c], nx_s.at[slot], nx_r.at[slot], py, pz - 1,
               gate=passed(pz, g), away=True)

    def result_sends(k, do):
        y = wrap(py + k)
        for z in range(count_z):
            slot = k * count_z + z
            two = inner * (1 - passed(pz, z))
            do(result.at[:, band(z), cols(y)], got.at[me], a_s.at[slot], a_r.at[me], y, z, gate=two)
            do(result.at[1, band(z), cols(y)], got.at[me, 1], a_s.at[slot], a_r.at[me], y, z, gate=1 - two)

    for j in range(min(AHEAD, count_y)):
        pressure_sends(j, begin)
    for k in range(min(AHEAD_F, count_y)):
        fluid_sends(k, begin)
    for load in loads:
        load.wait()

    def tile_at(c):
        return pl.ds(pl.multiple_of(c * width + (width - LANES), LANES), LANES)

    def before(tile, values):
        wide = jnp.concatenate([tile, values], 1)
        return pltpu.roll(wide, 1, 1)[:, LANES:]

    def project(k):
        y = wrap(py + k)
        c = cols(y)

        @pl.when(me > 0)
        def _():
            landed(f_low.at[:, c], f_r.at[k])

        fluid = f[:, c]
        here = press[1, :, c]
        w_x = 0.5 * (fluid + f_low[:, c])
        along_x = w_x * (v[0, :, c] - (here - press[0, :, c]))
        along_x = jnp.where(me == 0, jnp.float32(0.0), along_x)
        out[0, :, c] = along_x
        result[0, :, c] = along_x
        lend(k, begin)
        z_index = lax.broadcasted_iota(jnp.int32, fluid.shape, 0)
        w_z = 0.5 * (fluid + pltpu.roll(fluid, 1, 0))
        along_z = w_z * (v[1, :, c] - (here - pltpu.roll(here, 1, 0)))
        out[1, :, c] = jnp.where(z_index == 0, jnp.float32(0.0), along_z)
        y_index = lax.broadcasted_iota(jnp.int32, fluid.shape, 1) + y * width
        tile = tile_at(wrap(y - 1))
        w_y = 0.5 * (fluid + before(f[:, tile], fluid))
        along_y = w_y * (v[2, :, c] - (here - before(press[1, :, tile], here)))
        out[2, :, c] = jnp.where(y_index == 0, jnp.float32(0.0), along_y)

    def diverge(k):
        y = wrap(py + k)
        c = cols(y)
        along_z = out[1, :, c]
        along_y = out[2, :, c]
        z_index = lax.broadcasted_iota(jnp.int32, along_z.shape, 0)
        y_index = lax.broadcasted_iota(jnp.int32, along_z.shape, 1) + y * width
        z_next = jnp.where(z_index == rows - 1, jnp.float32(0.0), pltpu.roll(along_z, rows - 1, 0))
        tile = out[2, :, pl.ds(pl.multiple_of(wrap(y + 1) * width, width), LANES)]
        wide = pltpu.roll(jnp.concatenate([along_y, tile], 1), width + LANES - 1, 1)[:, :width]
        y_next = jnp.where(y_index == across - 1, jnp.float32(0.0), wide)
        result[1, :, c] = (z_next - along_z) + (y_next - along_y) - out[0, :, c]

        for g in range(count_z):
            @pl.when(passed_up(pz, g) > 0)
            def _():
                landed(next_x.at[band(g), c], nx_r.at[k * count_z + g])
                result[1, band(g), c] = result[1, band(g), c] + next_x[band(g), c]

        result_sends(k, begin)

    def store(q, z):
        added = clip(planes - 1 - q) * (1 - passed_up(z, pz))

        @pl.when(added > 0)
        def _():
            div[q] = got[q, 1] + got[jnp.minimum(q + 1, planes - 1), 0]

        @pl.when(added <= 0)
        def _():
            div[q] = got[q, 1]

    def collect(k):
        y = wrap(py - k)
        for z in range(count_z):
            q = y * count_z + z
            two = clip(q) * (1 - passed(z, pz))
            landed(got.at[q], a_r.at[q], two)
            landed(got.at[q, 1], a_r.at[q], 1 - two)
        for z in range(last):
            store(y * count_z + z, z)

        @pl.when(k > 0)
        def _():
            store(y * count_z + last, last)

    arrive(0)
    ready(0)
    if count_y > 1:
        arrive(1)

    def step(k, carry):
        @pl.when(k + AHEAD < count_y)
        def _():
            pressure_sends(k + AHEAD, begin)

        @pl.when(k + AHEAD_F < count_y)
        def _():
            fluid_sends(k + AHEAD_F, begin)

        @pl.when(k >= LATE)
        def _():
            diverge(k - LATE)

        @pl.when(k + 2 < count_y)
        def _():
            arrive(k + 2)

        @pl.when(k + 1 < count_y)
        def _():
            ready(k + 1)

        @pl.when(k < count_y)
        def _():
            project(k)

        @pl.when(k >= LAG)
        def _():
            collect(k - LAG)
        return carry

    lax.fori_loop(0, count_y + LATE, step, 0)

    def finish(k, carry):
        pressure_sends(k, sent)
        fluid_sends(k, sent)
        for g in range(count_z):
            lift(k, g, sent)
            drop(k, g, sent)
        lend(k, sent)
        result_sends(k, sent)
        return carry

    lax.fori_loop(0, count_y, finish, 0)

    def rest(k, carry):
        collect(k)
        return carry

    lax.fori_loop(max(count_y + LATE - LAG, 0), count_y, rest, 0)
    store(me - pz + last, last)


def write_out(updated, total, updated_hbm, total_hbm, sem):
    rows, planes = updated.shape[2] // PIECES, total.shape[0] // PIECES
    copies = []
    for i in range(PIECES):
        for d in range(3):
            part = (d, 0, pl.ds(i * rows, rows))
            copies.append(pltpu.make_async_copy(updated.at[part], updated_hbm.at[part], sem.at[len(copies)]))
        part = pl.ds(i * planes, planes)
        copies.append(pltpu.make_async_copy(total.at[part], total_hbm.at[part], sem.at[len(copies)]))
    for copy in copies:
        copy.start()
    for copy in copies:
        copy.wait()


def on_device(velocity, fluid, pressure):
    count_y = lax.axis_size("py")
    count_z = lax.axis_size("pz")
    rows, across = fluid.shape[1:]
    planes = pressure.shape[0]
    block = pressure.shape[1:]
    vm = lambda *shape: pltpu.VMEM(shape, jnp.float32)
    dma = lambda n: pltpu.SemaphoreType.DMA((n,))
    steps = count_y * count_z
    updated, total = pl.pallas_call(
        functools.partial(kernel, count_y, count_z),
        out_shape=(
            jax.ShapeDtypeStruct(velocity.shape, jnp.float32),
            jax.ShapeDtypeStruct(pressure.shape, jnp.float32),
        ),
        in_specs=[pl.BlockSpec(memory_space=pltpu.MemorySpace.HBM)] * 3,
        out_specs=(pl.BlockSpec(memory_space=pltpu.VMEM),) * 2,
        scratch_shapes=[
            vm(3, rows, across), vm(rows, across), vm(rows, across), vm(2, rows, across), vm(2, rows, across),
            vm(rows, across), vm(planes, 2, *block), dma(2),
            dma(steps), dma(steps), dma(steps), dma(steps), dma(steps),
            dma(count_y), dma(count_y), dma(steps), dma(steps), dma(steps), dma(planes),
        ],
        compiler_params=pltpu.CompilerParams(
            collective_id=0, has_side_effects=True, vmem_limit_bytes=40 << 20
        ),
        name="project_all",
    )(*(pltpu.with_memory_space_constraint(x, pltpu.MemorySpace.HBM) for x in (velocity, fluid, pressure)))
    return pl.pallas_call(
        write_out,
        out_shape=(
            jax.ShapeDtypeStruct(velocity.shape, jnp.float32),
            jax.ShapeDtypeStruct(pressure.shape, jnp.float32),
        ),
        in_specs=[pl.BlockSpec(memory_space=pltpu.VMEM)] * 2,
        out_specs=(pl.BlockSpec(memory_space=pltpu.MemorySpace.HBM),) * 2,
        scratch_shapes=[dma(PIECES * 4)],
        compiler_params=pltpu.CompilerParams(vmem_limit_bytes=40 << 20),
        name="write_out",
    )(updated, total)


def solution(mesh):
    placed = (P(None, ("py", "pz"), None, None), P(("py", "pz"), None, None), P(None, "pz", "py"))
    return jax.shard_map(
        on_device,
        mesh=mesh,
        in_specs=placed,
        out_specs=(P(None, ("py", "pz"), None, None), P(None, "pz", "py")),
        check_vma=False,
    )
```
